128 devices in a mesh: tm: 32 (over x, y, z_hi), tensor: 4 (over z_lo, core).
Axes of the slice: x: 4, y: 4, z: 4 (z_hi: 2, z_lo: 2; z = z_hi * 2 + z_lo), core: 2. Of those that a mesh axis runs over, the one named last changes fastest.
Arguments:
- frames: bfloat16 [16384, 1408], P('tm'), may hold values from -6 to 6
- gain_attn: float32 [1408], replicated, may hold values from 0.25 to 1.75
- w_qkv: bfloat16 [1408, 3, 1408], P('tm', None, 'tensor')
- w_out: bfloat16 [1408, 1408], P('tensor', 'tm'), may hold values from -0.625 to 0.625
- gain_mlp: float32 [1408], replicated, may hold values from 0.25 to 1.75
- w_up: bfloat16 [1408, 6144], P('tm', 'tensor'), may hold values from -0.15625 to 0.15625
- w_down: bfloat16 [6144, 1408], P('tensor', 'tm'), may hold values from -0.078125 to 0.078125
- w_proj: bfloat16 [1408, 4096], P('tm', 'tensor'), may hold values from -0.15625 to 0.15625
- windows: int32 [256, 8], P('tm'), may hold values from 0 to 255, as said below
- pool_map: int32 [16384], P('tm'), may hold values from 0 to 15, as said below
- owners: int32 [4096, 1], P('tm'), may hold values from 0 to 31; in each aligned block of 128 rows (0 to 127, 128 to 255, ...) at most 8 rows name the same one
Outputs:
- received: bfloat16 [32, 256, 4096], P('tm', None, 'tensor')
The draws below stay inside these ranges and needn't reach their ends.
Inputs may be any that keep to these rules, and one draw needn't show every extreme that they name: `windows`: row b lists 8 different blocks, each in the frame of block b or in the frame just before or just after it; frame f holds blocks 256 / 64 f onward. `pool_map`: in each aligned block of 64 patches every slot value is named by exactly 4 patches. `owners`: among the 128 rows of one index of tm no owner is named more than 8 times.
All inputs are finite; a program needn't handle non-finite values.
Results may differ from the reference program's by a relative error of at most 0.014.
The reference program's roundings to bfloat16 on the way count: a program that leaves them out, or rounds other values in their place, can miss the bound.
Values may be sent and summed in bfloat16 or wider, within the bound.
A program may use at most 64 MiB of HBM per device.

```python
import math
import jax
import jax.numpy as jnp
import numpy as np
from jax import lax

D = 1408
HEADS = 16
FF = 6144
LLM_D = 4096
PATCHES = 256
BLK = 64
WIN = 8
POOL = 4
NF = 64
TOKENS = 16384
NBLK = 256
POOLED = 4096
CAP = 8
N_TM = 32
N_TENSOR = 4


def draw_w_qkv(key, part):
    base = jax.random.normal(jax.random.fold_in(key, 1), (D, 3, D), jnp.float32) * D ** (-0.5)
    return base.astype(jnp.bfloat16)


def draw_windows(key, part):
    per_frame = PATCHES // BLK
    block_ids = jnp.arange(NBLK, dtype=jnp.int32)
    frame_ids = block_ids // per_frame
    offsets = jnp.arange(3 * per_frame, dtype=jnp.int32)
    cand_frames = frame_ids[:, None] - 1 + offsets[None, :] // per_frame
    candidates = cand_frames * per_frame + offsets[None, :] % per_frame
    invalid = ((cand_frames < 0) | (cand_frames >= NF)).astype(jnp.int32)
    priority = jax.vmap(lambda row_key: jax.random.permutation(row_key, 3 * per_frame))(jax.random.split(jax.random.fold_in(key, 3), NBLK))
    ranking = jnp.argsort(priority.astype(jnp.int32) + 100 * invalid, axis=1, stable=True)
    return jnp.take_along_axis(candidates, ranking[:, :WIN], axis=1).astype(jnp.int32)


def draw_pool_map(key, part):
    block_count = TOKENS // BLK
    orders = jax.vmap(lambda row_key: jax.random.permutation(row_key, BLK))(jax.random.split(jax.random.fold_in(key, 4), block_count))
    inverse = jnp.argsort(orders.astype(jnp.int32), axis=1, stable=True)
    return (inverse // POOL).reshape(TOKENS).astype(jnp.int32)


def levels(stream_key, dims, cuts, low, top_value):
    gain, own = 1.0, jax.random.fold_in(stream_key, 6)
    for dim, blocks in cuts:
        draws = jnp.exp(jax.random.uniform(jax.random.fold_in(own, dim), (blocks,), jnp.float32, low / len(cuts), top_value / len(cuts)))
        gain = gain * jnp.repeat(draws, dims[dim] // blocks).reshape([-1 if axis == dim else 1 for axis in range(len(dims))])
    return gain


def routed_block(rng, own, number, rows, amount, top, most, slope):
    order = jax.random.permutation(rng, amount)
    heavy_load, ordinary = portions_of(amount, rows * top, most, slope, True), portions_of(amount, rows * top, most, slope, False)
    places = jnp.arange(amount)

    def named(sizes, rotation):
        used = int((sizes > 0).sum())
        fixed = max(1, used // 4)
        shifted = fixed + (places - fixed + rotation * (used - fixed)) % max(1, amount - fixed)
        return jnp.zeros((amount,), jnp.int32).at[order[jnp.where(places < fixed, places, shifted)]].set(jnp.asarray(sizes, jnp.int32))

    sizes = jnp.where(number % 4 == 0, named(heavy_load, number // 4), named(ordinary, number - number // 4 - 1))
    mixed = jax.random.permutation(jax.random.fold_in(own, 3), amount)
    donor, taker = mixed[0:amount // 2 * 2:2], mixed[1:amount // 2 * 2:2]
    slack = jnp.minimum(sizes[donor] - 1, most - sizes[taker]) // 2
    slack = jnp.where((donor == order[0]) | (taker == order[0]) | (sizes[taker] == 0), 0, jnp.maximum(slack, 0))
    shifted = jax.random.randint(jax.random.fold_in(own, 4), (amount // 2,), 0, 1 << 20) % (slack + 1)
    sizes = sizes.at[donor].add(-shifted).at[taker].add(shifted)
    members = jnp.searchsorted(jnp.cumsum(sizes), jnp.arange(rows * top), side="right").astype(jnp.int32)
    grid = members.reshape(top, rows).T
    grid = grid[jax.random.permutation(jax.random.fold_in(own, 1), rows)]
    rotation = jax.random.randint(jax.random.fold_in(own, 2), (rows, 1), 0, top)
    return jnp.take_along_axis(grid, (jnp.arange(top)[None, :] + rotation) % top, axis=1)


def portions_of(count, total, bound, skew, full):
    loads = [(1 << 20) // math.isqrt(standing ** skew) + 1 for standing in range(1, count + 1)]
    largest = bound if full else min(bound, max(-(-total // count), total * loads[0] // sum(loads)))
    least = 1 if total - largest >= count - 1 else 0
    counts, rest = [largest] + [least] * (count - 1), total - largest - least * (count - 1)
    while rest > 0:
        free = [i for i in range(1, count) if counts[i] < largest] or [i for i in range(1, count) if counts[i] < bound]
        whole, budget = sum([loads[i] for i in free]), rest
        for i in free:
            addition = min(bound - counts[i], max(1, budget * loads[i] // whole), rest)
            counts[i] = counts[i] + addition
            rest = rest - addition
    return np.array(counts)


def noise(stream_key, shape, scale, limit, cuts=(), kind=jnp.bfloat16):
    factor_of = levels(stream_key, shape, cuts, -0.22, 0.18) if cuts else 1.0
    entries = jax.random.normal(stream_key, shape, jnp.float32) * scale * factor_of
    return jnp.minimum(jnp.maximum(entries, -limit), limit).astype(kind)


def setup_inputs(seed: int = 0) -> dict:
    key_list = jax.random.split(jax.random.key(seed), 12)
    frames = noise(key_list[0], (TOKENS, D), 1.0, 6.0, ((0, 32),))
    gain_attn = jnp.clip(1.0 + 0.15 * jax.random.normal(key_list[1], (D,), jnp.float32), 0.25, 1.75)
    w_qkv = draw_w_qkv(jax.random.fold_in(key_list[11], 71), 0)
    w_out = noise(key_list[3], (D, D), (D // 16) ** -0.5, 0.625, ((0, 4), (1, 32)))
    gain_mlp = jnp.clip(1.0 + 0.15 * jax.random.normal(key_list[4], (D,), jnp.float32), 0.25, 1.75)
    w_up = noise(key_list[5], (D, FF), D ** -0.5, 0.15625, ((0, 32), (1, 4)))
    w_down = noise(key_list[6], (FF, D), FF ** -0.5, 0.078125, ((0, 4), (1, 32)))
    w_proj = noise(key_list[7], (D, LLM_D), D ** -0.5, 0.15625, ((0, 32), (1, 4)))
    windows = draw_windows(jax.random.fold_in(key_list[11], 71), 0)
    pool_map = draw_pool_map(jax.random.fold_in(key_list[11], 71), 0)
    owners_keys = jax.random.split(jax.random.fold_in(key_list[10], 1), POOLED // (POOLED // N_TM))
    owners_turns = jax.random.permutation(jax.random.fold_in(key_list[10], 3), POOLED // (POOLED // N_TM))
    owners = jax.vmap(lambda own, number: routed_block(jax.random.fold_in(key_list[10], 2), own, number, POOLED // N_TM, N_TM, 1, CAP, 2))(owners_keys, owners_turns).reshape((POOLED, 1))
    return dict(frames=frames, gain_attn=gain_attn, w_qkv=w_qkv, w_out=w_out, gain_mlp=gain_mlp, w_up=w_up, w_down=w_down, w_proj=w_proj, windows=windows, pool_map=pool_map, owners=owners)


eps = 1e-06

def layer_norm(values, scales):
    average = lax.optimization_barrier(jnp.mean(values, axis=-1, keepdims=True))
    centred = values - average
    spread = lax.optimization_barrier(jnp.mean(centred * centred, axis=-1, keepdims=True))
    return (centred * lax.rsqrt(spread + eps) * scales).astype(jnp.bfloat16)

def pool_rows(values, slot_map):
    block_count = values.shape[0] // BLK
    slot_ids = jnp.arange(BLK // POOL, dtype=jnp.int32)
    chooser = (slot_map.reshape(block_count, 1, BLK) == slot_ids[None, :, None]).astype(jnp.float32)
    summed = jnp.einsum('bsp,bpd->bsd', chooser, values.reshape(block_count, BLK, values.shape[1]), precision=lax.Precision.HIGHEST)
    return (summed * (1.0 / POOL)).reshape(block_count * (BLK // POOL), values.shape[1]).astype(jnp.bfloat16)

def group_sum(operand, weight_rows):
    col_width = operand.shape[1] // N_TENSOR
    summed = jnp.zeros((operand.shape[0], weight_rows.shape[1]), jnp.float32)
    for member in range(N_TENSOR):
        term = jnp.dot(operand[:, member * col_width:(member + 1) * col_width], weight_rows[member * col_width:(member + 1) * col_width], preferred_element_type=jnp.float32)
        summed = summed + lax.optimization_barrier(term.astype(jnp.bfloat16)).astype(jnp.float32)
    return summed

def reference(frames, gain_attn, w_qkv, w_out, gain_mlp, w_up, w_down, w_proj, windows, pool_map, owners):
    head_dim = D // HEADS
    normed = layer_norm(frames.astype(jnp.float32), gain_attn)
    projected_qkv = jnp.dot(normed, w_qkv.reshape(D, 3 * D), preferred_element_type=jnp.float32).astype(jnp.bfloat16)
    all_blocks = projected_qkv.reshape(NBLK, BLK, 3, HEADS, head_dim)
    key_blocks = all_blocks[:, :, 1]
    value_blocks = all_blocks[:, :, 2]
    group_size = math.gcd(NBLK, 32)
    score_scale = head_dim ** (-0.5)

    def attend_group(packed):
        query_group, id_group = packed
        picked_keys = key_blocks[id_group].reshape(group_size, WIN * BLK, HEADS, head_dim).astype(jnp.float32)
        picked_values = value_blocks[id_group].reshape(group_size, WIN * BLK, HEADS, head_dim).astype(jnp.float32)
        scores = jnp.einsum('gqhd,gkhd->ghqk', query_group.astype(jnp.float32), picked_keys) * score_scale
        row_top = lax.optimization_barrier(jnp.max(scores, axis=-1, keepdims=True))
        expw = jnp.exp(scores - row_top)
        attn_probs = (expw / lax.optimization_barrier(jnp.sum(expw, axis=-1, keepdims=True))).astype(jnp.bfloat16)
        return jnp.einsum('ghqk,gkhd->gqhd', attn_probs.astype(jnp.float32), picked_values).astype(jnp.bfloat16)
    queries = all_blocks[:, :, 0].reshape(NBLK // group_size, group_size, BLK, HEADS, head_dim)
    attended = lax.map(attend_group, (queries, windows.reshape(NBLK // group_size, group_size, WIN))).reshape(TOKENS, D)
    row_block = math.gcd(TOKENS, 4096)

    def finish(packed):
        frame_rows, attended_rows, slot_rows = packed
        stream = frame_rows.astype(jnp.float32) + group_sum(attended_rows, w_out)
        hidden = layer_norm(stream, gain_mlp)
        activation = jax.nn.gelu(jnp.dot(hidden, w_up, preferred_element_type=jnp.float32), approximate=False).astype(jnp.bfloat16)
        stream = stream + group_sum(activation, w_down)
        return pool_rows(stream, slot_rows)
    pooled = lax.map(finish, (frames.reshape(TOKENS // row_block, row_block, D), attended.reshape(TOKENS // row_block, row_block, D), pool_map.reshape(TOKENS // row_block, row_block))).reshape(POOLED, D)
    proj_rows = jnp.dot(pooled, w_proj, preferred_element_type=jnp.float32).astype(jnp.bfloat16)
    per_source = POOLED // N_TM
    owner_ids = owners[:, 0].astype(jnp.int32)
    owner_hits = (owner_ids[:, None] == jnp.arange(N_TM, dtype=jnp.int32)[None, :]).astype(jnp.int32)
    running = jnp.cumsum(owner_hits.reshape(N_TM, per_source, N_TM), axis=1).astype(jnp.int32).reshape(POOLED, N_TM)
    slot_rank = lax.optimization_barrier(jnp.sum((running - 1) * owner_hits, axis=1)).astype(jnp.int32)
    source_ids = jnp.arange(POOLED, dtype=jnp.int32) // per_source
    slot_dest = (owner_ids * (N_TM * CAP) + source_ids * CAP + slot_rank).astype(jnp.int32)
    received = jnp.zeros((N_TM * N_TM * CAP, LLM_D), jnp.bfloat16).at[slot_dest].set(proj_rows)
    return received.reshape(N_TM, N_TM * CAP, LLM_D)
```

```python
import functools
import math

import jax
import jax.numpy as jnp
from jax import lax
from jax.experimental import pallas as pl
from jax.experimental.pallas import tpu as pltpu
from jax.sharding import PartitionSpec as P

D = 1408
HEADS = 16
PATCHES = 256
BLK = 64
WIN = 8
POOL = 4
N_TM = 32
ROWS = D // N_TM
PROWS = 48
DP = N_TM * PROWS

eps = 1e-06
MESH = pl.DeviceIdType.MESH
OFFSETS = (0, -1, 1, 2)
N_EVENTS = 20


class RingGather:
    def __init__(self, own, bufs, send_sems, recv_sems, local_sems, z_sems):
        self.own, self.bufs = own, bufs
        self.send_sems, self.recv_sems = send_sems, recv_sems
        self.local_sems, self.z_sems = local_sems, z_sems
        self.tm = lax.axis_index("tm")
        self.t = lax.axis_index("tensor")
        self.x = self.tm // 8
        self.y = (self.tm // 2) % 4
        self.zh = self.tm % 2

    def colour(self, fam):
        return self.zh if fam == 0 else 1 - self.zh

    def at(self, fam, a, b, z):
        k = self.colour(fam)
        dx = a * (1 - k) + b * k
        dy = a * k + b * (1 - k)
        return (((self.x + dx + 4) % 4) * 4 + (self.y + dy + 4) % 4) * 2 + z

    def device(self, fam, a, b):
        return (self.at(fam, a, b, self.zh), self.t)

    def part(self, c, fam, a, b, half):
        buf = self.bufs[c]
        slot = self.at(fam, a, b, self.colour(fam))
        if half is None:
            return buf.at[slot]
        n = buf.shape[2]
        cut = (n // 2 + 127) // 128 * 128
        return buf.at[slot, :, pl.ds(0, cut) if half == 0 else pl.ds(cut, n - cut)]

    def event(self, c, fam, ev):
        if ev < 4:
            a, b, half, da, db = ((0, 0, None, 1, 0), (0, 0, None, -1, 0), (-1, 0, 0, 1, 0), (1, 0, 1, -1, 0))[ev]
        else:
            off = OFFSETS[(ev - 4) // 4]
            a, b, half, da, db = (
                (off, 0, None, 0, 1), (off, 0, None, 0, -1), (off, -1, 0, 0, 1), (off, 1, 1, 0, -1)
            )[(ev - 4) % 4]
        src = self.part(c, fam, a, b, half)
        if fam == 0 and a == 0 and b == 0:
            src = self.own[c]
        dst = self.part(c, fam, a, b, half)
        landed = self.part(c, fam, a - da if a - da > -2 else 2, b - db if b - db > -2 else 2, half)
        sem = (c * 2 + fam) * N_EVENTS + ev
        return src, dst, landed, sem, self.device(fam, da, db)

    def start(self, c, fam, *events):
        for ev in events:
            src, dst, _, sem, dev = self.event(c, fam, ev)
            pltpu.make_async_remote_copy(
                src_ref=src, dst_ref=dst, send_sem=self.send_sems.at[sem], recv_sem=self.recv_sems.at[sem],
                device_id=dev, device_id_type=MESH,
            ).start()

    def wait(self, c, fam, *events):
        for ev in events:
            _, _, landed, sem, dev = self.event(c, fam, ev)
            pltpu.make_async_remote_copy(
                src_ref=landed, dst_ref=landed, send_sem=self.send_sems.at[sem], recv_sem=self.recv_sems.at[sem],
                device_id=dev, device_id_type=MESH,
            ).wait_recv()

    def wait_sends(self):
        for c in range(len(self.own)):
            for fam in range(2):
                for ev in range(N_EVENTS):
                    src, dst, _, sem, dev = self.event(c, fam, ev)
                    pltpu.make_async_remote_copy(
                        src_ref=src, dst_ref=dst, send_sem=self.send_sems.at[sem], recv_sem=self.recv_sems.at[sem],
                        device_id=dev, device_id_type=MESH,
                    ).wait_send()
            self.z_copy(c, self.tm).wait_send()

    def z_copy(self, c, slot):
        partner = self.tm + 1 - 2 * self.zh
        return pltpu.make_async_remote_copy(
            src_ref=self.own[c], dst_ref=self.bufs[c].at[slot],
            send_sem=self.z_sems.at[0, c], recv_sem=self.z_sems.at[1, c],
            device_id=(partner, self.t), device_id_type=MESH,
        )

    def local(self, c):
        return pltpu.make_async_copy(self.own[c], self.bufs[c].at[self.tm], self.local_sems.at[c])

    def barrier(self):
        sem = pltpu.get_barrier_semaphore()
        devs = [self.device(0, 1, 0), self.device(0, -1, 0), self.device(0, 0, 1), self.device(0, 0, -1),
                (self.tm + 1 - 2 * self.zh, self.t)]
        for dev in devs:
            pl.semaphore_signal(sem, inc=1, device_id=dev, device_id_type=MESH)
        pl.semaphore_wait(sem, len(devs))

    def stage(self, c, s):
        if s == 0:
            self.z_copy(c, self.tm).start()
            self.start(c, 0, 0, 1, 4, 5)
            self.local(c).start()
        elif s == 1:
            self.z_copy(c, self.tm + 1 - 2 * self.zh).wait_recv()
            self.start(c, 1, 0, 1, 4, 5)
            self.local(c).wait()
        elif s < 6:
            for fam in range(2):
                if s == 2:
                    self.wait(c, fam, 0)
                    self.start(c, fam, 2, 8, 9)
                    self.wait(c, fam, 1)
                    self.start(c, fam, 3, 12, 13)
                    for ev in (4, 5):
                        self.wait(c, fam, ev)
                        self.start(c, fam, ev + 2)
                elif s == 3:
                    self.wait(c, fam, 2, 3)
                    self.start(c, fam, 16, 17)
                    for ev in (8, 9, 12, 13):
                        self.wait(c, fam, ev)
                        self.start(c, fam, ev + 2)
                elif s == 4:
                    for ev in (16, 17):
                        self.wait(c, fam, ev)
                        self.start(c, fam, ev + 2)
                else:
                    self.wait(c, fam, 6, 7, 10, 11, 14, 15, 18, 19)


def gather_kernel(n, *refs):
    own, bufs, sems = refs[:n], refs[n:2 * n], refs[2 * n:]
    g = RingGather(own, bufs, *sems)
    g.barrier()
    for tick in range(n + 5):
        for c in range(n):
            if 0 <= tick - c < 6:
                g.stage(c, tick - c)
    g.wait_sends()


def gather_weights(parts):
    n = len(parts)
    vmem = pl.BlockSpec(memory_space=pltpu.VMEM)
    return pl.pallas_call(
        functools.partial(gather_kernel, n),
        out_shape=[jax.ShapeDtypeStruct((N_TM, PROWS, p.shape[1]), jnp.bfloat16) for p in parts],
        in_specs=[vmem] * n,
        out_specs=[vmem] * n,
        scratch_shapes=[
            pltpu.SemaphoreType.DMA((n * 2 * N_EVENTS,)),
            pltpu.SemaphoreType.DMA((n * 2 * N_EVENTS,)),
            pltpu.SemaphoreType.DMA((n,)),
            pltpu.SemaphoreType.DMA((2, n)),
        ],
        compiler_params=pltpu.CompilerParams(collective_id=0, has_side_effects=True, vmem_limit_bytes=60 << 20),
    )(*parts)


def with_halo(block, sides, width):
    for axis, dim in sides:
        count = lax.axis_size(axis)
        forward = [(i, i + 1) for i in range(count - 1)]
        backward = [(target, source) for source, target in forward]
        low = lax.ppermute(
            lax.slice_in_dim(block, block.shape[dim] - width, None, axis=dim), axis, forward
        )
        high = lax.ppermute(lax.slice_in_dim(block, 0, width, axis=dim), axis, backward)
        block = jnp.concatenate([low, block, high], axis=dim)
    return block


def pad_features(values):
    src = jnp.arange(D, dtype=jnp.int32)
    place = (src // ROWS * PROWS + src % ROWS)[:, None] == jnp.arange(DP, dtype=jnp.int32)[None, :]
    return jnp.dot(values, place.astype(values.dtype), preferred_element_type=jnp.float32)


def pad_gain(gain):
    return jnp.pad(gain.reshape(N_TM, ROWS), ((0, 0), (0, PROWS - ROWS))).reshape(1, DP)


def layer_norm(values, scales):
    real = (jnp.arange(DP, dtype=jnp.int32) % PROWS < ROWS).astype(jnp.float32)[None, :]
    average = jnp.sum(values, axis=-1, keepdims=True) * (1.0 / D)
    centred = (values - average) * real
    spread = jnp.sum(centred * centred, axis=-1, keepdims=True) * (1.0 / D)
    return (centred * lax.rsqrt(spread + eps) * scales).astype(jnp.bfloat16)


def pool_rows(values, slot_map):
    block_count = values.shape[0] // BLK
    slot_ids = jnp.arange(BLK // POOL, dtype=jnp.int32)
    chooser = (slot_map.reshape(block_count, 1, BLK) == slot_ids[None, :, None]).astype(jnp.float32)
    summed = jnp.einsum(
        "bsp,bpd->bsd",
        chooser,
        values.reshape(block_count, BLK, values.shape[1]),
        precision=lax.Precision.HIGHEST,
    )
    return (
        (summed * (1.0 / POOL))
        .reshape(block_count * (BLK // POOL), values.shape[1])
        .astype(jnp.bfloat16)
    )


def tensor_total(term):
    return lax.psum(term.astype(jnp.bfloat16), "tensor").astype(jnp.float32)


def nt_dot(a, b):
    return lax.dot_general(a, b, (((1,), (1,)), ((), ())), preferred_element_type=jnp.float32)


def body(
    frames, gain_attn, w_qkv, w_out, gain_mlp, w_up, w_down, w_proj, windows, pool_map, owners
):
    row_count = frames.shape[0]
    query_blocks = row_count // BLK
    head_dim = D // HEADS
    local_width = w_qkv.shape[2]
    pad = lambda w: jnp.pad(w, ((0, PROWS - ROWS), (0, 0)))
    parts = [
        pad(w_qkv.reshape(ROWS, 3 * local_width)), pad(w_out.T), pad(w_up), pad(w_down.T), pad(w_proj)
    ]
    full_qkv, full_out_t, full_up, full_down_t, full_proj = [
        w.reshape(DP, w.shape[2]) for w in gather_weights(parts)
    ]
    heads_here = local_width // head_dim
    frames_wide = pad_features(frames)
    normed = layer_norm(frames_wide, pad_gain(gain_attn))
    projected_qkv = jnp.dot(normed, full_qkv, preferred_element_type=jnp.float32).astype(jnp.bfloat16)
    projected_qkv = projected_qkv.reshape(row_count, 3, local_width)
    keyvals = with_halo(projected_qkv[:, 1:, :], (("tm", 0),), PATCHES)
    per_frame = PATCHES // BLK
    kv_blocks = keyvals.reshape(query_blocks + 2 * per_frame, BLK, 2, heads_here, head_dim)
    local_ids = windows - (lax.axis_index("tm") * query_blocks - per_frame)
    group_size = math.gcd(query_blocks, 8)
    queries = projected_qkv[:, 0, :].reshape(
        query_blocks // group_size, group_size, BLK, heads_here, head_dim
    )
    score_scale = head_dim ** (-0.5)

    def attend_group(packed):
        query_group, id_group = packed
        picked = kv_blocks[id_group].reshape(group_size, WIN * BLK, 2, heads_here, head_dim)
        scores = (
            jnp.einsum(
                "gqhd,gkhd->ghqk", query_group, picked[:, :, 0], preferred_element_type=jnp.float32
            )
            * score_scale
        )
        row_top = jnp.max(scores, axis=-1, keepdims=True)
        expw = jnp.exp(scores - row_top)
        attn_probs = (expw / jnp.sum(expw, axis=-1, keepdims=True)).astype(jnp.bfloat16)
        return jnp.einsum(
            "ghqk,gkhd->gqhd", attn_probs, picked[:, :, 1], preferred_element_type=jnp.float32
        ).astype(jnp.bfloat16)

    attended = lax.map(
        attend_group, (queries, local_ids.reshape(query_blocks // group_size, group_size, WIN))
    ).reshape(row_count, local_width)
    mixed_term = nt_dot(attended, full_out_t)
    stream = frames_wide + tensor_total(mixed_term)
    hidden = layer_norm(stream, pad_gain(gain_mlp))
    activation = jax.nn.gelu(
        jnp.dot(hidden, full_up, preferred_element_type=jnp.float32), approximate=False
    ).astype(jnp.bfloat16)
    stream = stream + tensor_total(nt_dot(activation, full_down_t))
    pooled = pool_rows(stream, pool_map)
    proj_rows = jnp.dot(pooled, full_proj, preferred_element_type=jnp.float32).astype(jnp.bfloat16)
    pooled_count = proj_rows.shape[0]
    owner_count = lax.axis_size("tm")
    capacity = 2 * pooled_count // owner_count
    owner_ids = owners[:, 0]
    owner_hits = (owner_ids[:, None] == jnp.arange(owner_count, dtype=jnp.int32)[None, :]).astype(
        jnp.int32
    )
    slot_rank = jnp.sum((jnp.cumsum(owner_hits, axis=0) - 1) * owner_hits, axis=1)
    slot_dest = owner_ids * capacity + slot_rank
    placement = (
        jnp.arange(owner_count * capacity, dtype=jnp.int32)[:, None] == slot_dest[None, :]
    ).astype(jnp.bfloat16)
    outbox = jnp.dot(placement, proj_rows, preferred_element_type=jnp.float32).astype(jnp.bfloat16)
    outbox = outbox.reshape(owner_count, capacity, proj_rows.shape[1])
    received = lax.all_to_all(outbox, "tm", split_axis=0, concat_axis=0, tiled=True)
    return received.reshape(1, owner_count * capacity, proj_rows.shape[1])


def solution(mesh):
    placed = (
        P("tm", None),
        P(),
        P("tm", None, "tensor"),
        P("tensor", "tm"),
        P(),
        P("tm", "tensor"),
        P("tensor", "tm"),
        P("tm", "tensor"),
        P("tm", None),
        P("tm"),
        P("tm", None),
    )
    return jax.shard_map(
        body, mesh=mesh, in_specs=placed, out_specs=P("tm", None, "tensor"), check_vma=False
    )
```

```python
import functools

import jax
import jax.numpy as jnp
from jax import lax
from jax.experimental import pallas as pl
from jax.experimental.pallas import tpu as pltpu
from jax.sharding import PartitionSpec as P

D = 1408
HEADS = 16
PATCHES = 256
BLK = 64
WIN = 8
POOL = 4
N_TM = 32
HEAD_DIM = D // HEADS
HERE = 4
HW = 384
ROWS = D // N_TM
PROWS = 48
DP = N_TM * PROWS
FF8 = 768
LM8 = 512
WIDTHS = (3 * HW, HW, FF8, FF8, LM8)
QKV, OUT, UP, DOWN, PROJ = range(5)
START = (0, 2, 4, 6, 8)

eps = 1e-06
MESH = pl.DeviceIdType.MESH
OFFSETS = (0, -1, 1, 2)
N_EVENTS = 20
F32 = jnp.float32
BF16 = jnp.bfloat16


class Place:
    def __init__(self):
        self.tm = lax.axis_index("tm")
        self.t = lax.axis_index("tensor")
        self.xy = self.tm // 2
        self.x = self.tm // 8
        self.y = self.xy % 4
        self.zh = self.tm % 2
        self.zl = self.t // 2
        self.c = self.t % 2
        self.z = self.zh * 2 + self.zl
        self.partner = self.tm + 1 - 2 * self.zh

    def ring(self, dz, c):
        z = (self.z + dz + 4) % 4
        return (self.xy * 2 + z // 2, (z % 2) * 2 + c)


class Copies:
    def __init__(self, send_sems, recv_sems):
        self.send_sems, self.recv_sems = send_sems, recv_sems
        self.used = 0
        self.sent = []

    def take(self, n=1):
        self.used += n
        return self.used - n

    def make(self, src, dst, sem, dev):
        return pltpu.make_async_remote_copy(
            src_ref=src, dst_ref=dst, send_sem=self.send_sems.at[sem], recv_sem=self.recv_sems.at[sem],
            device_id=dev, device_id_type=MESH,
        )

    def start(self, src, dst, sem, dev):
        copy = self.make(src, dst, sem, dev)
        copy.start()
        self.sent.append(copy)

    def arrived(self, landed, sem, dev):
        self.make(landed, landed, sem, dev).wait_recv()

    def drain(self):
        for copy in self.sent:
            copy.wait_send()
        self.sent = []


class RingGather:
    def __init__(self, place, copies, parts, bufs, local_sems):
        self.p, self.copies, self.parts, self.bufs, self.local_sems = place, copies, parts, bufs, local_sems
        self.base = [copies.take(2 * N_EVENTS + 1) for _ in parts]

    def own(self, c):
        return self.parts[c] if c < UP else self.parts[c].at[self.p.zh]

    def theirs(self, c):
        return self.parts[c] if c < UP else self.parts[c].at[1 - self.p.zh]

    def colour(self, fam):
        return self.p.zh if fam == 0 else 1 - self.p.zh

    def at(self, fam, a, b, z):
        k = self.colour(fam)
        dx = a * (1 - k) + b * k
        dy = a * k + b * (1 - k)
        return (((self.p.x + dx + 4) % 4) * 4 + (self.p.y + dy + 4) % 4) * 2 + z

    def part(self, c, fam, a, b, half):
        buf = self.bufs[c]
        slot = self.at(fam, a, b, self.colour(fam))
        if half is None:
            return buf.at[slot]
        n = buf.shape[2]
        cut = (n // 2 + 127) // 128 * 128
        return buf.at[slot, :, pl.ds(0, cut) if half == 0 else pl.ds(cut, n - cut)]

    def event(self, c, fam, ev):
        if ev < 4:
            a, b, half, da, db = ((0, 0, None, 1, 0), (0, 0, None, -1, 0), (-1, 0, 0, 1, 0), (1, 0, 1, -1, 0))[ev]
        else:
            off = OFFSETS[(ev - 4) // 4]
            a, b, half, da, db = (
                (off, 0, None, 0, 1), (off, 0, None, 0, -1), (off, -1, 0, 0, 1), (off, 1, 1, 0, -1)
            )[(ev - 4) % 4]
        dst = self.part(c, fam, a, b, half)
        src = self.own(c) if fam == 0 and a == 0 and b == 0 else dst
        landed = self.part(c, fam, a - da if a - da > -2 else 2, b - db if b - db > -2 else 2, half)
        sem = self.base[c] + fam * N_EVENTS + ev
        return src, dst, landed, sem, (self.at(fam, da, db, self.p.zh), self.p.t)

    def start(self, c, fam, *events):
        for ev in events:
            src, dst, _, sem, dev = self.event(c, fam, ev)
            self.copies.start(src, dst, sem, dev)

    def wait(self, c, fam, *events):
        for ev in events:
            _, _, landed, sem, dev = self.event(c, fam, ev)
            self.copies.arrived(landed, sem, dev)

    def stage(self, c, s):
        z_sem, z_dev = self.base[c] + 2 * N_EVENTS, (self.p.partner, self.p.t)
        if s < 2:
            local = pltpu.make_async_copy(self.own(c), self.bufs[c].at[self.p.tm], self.local_sems.at[c])
        if s == 0:
            self.copies.start(self.theirs(c), self.bufs[c].at[self.p.tm], z_sem, z_dev)
            self.start(c, 0, 0, 1, 4, 5)
            local.start()
        elif s == 1:
            self.copies.arrived(self.bufs[c].at[self.p.partner], z_sem, z_dev)
            self.start(c, 1, 0, 1, 4, 5)
            local.wait()
        else:
            for fam in range(2):
                if s == 2:
                    self.wait(c, fam, 0)
                    self.start(c, fam, 2, 8, 9)
                    self.wait(c, fam, 1)
                    self.start(c, fam, 3, 12, 13)
                    for ev in (4, 5):
                        self.wait(c, fam, ev)
                        self.start(c, fam, ev + 2)
                elif s == 3:
                    self.wait(c, fam, 2, 3)
                    self.start(c, fam, 16, 17)
                    for ev in (8, 9, 12, 13):
                        self.wait(c, fam, ev)
                        self.start(c, fam, ev + 2)
                elif s == 4:
                    for ev in (16, 17):
                        self.wait(c, fam, ev)
                        self.start(c, fam, ev + 2)
                else:
                    self.wait(c, fam, 6, 7, 10, 11, 14, 15, 18, 19)

    def tick(self, now):
        for c in range(5):
            if 0 <= now - START[c] < 6:
                self.stage(c, now - START[c])


class ZRing:
    def __init__(self, place, copies, buf):
        self.p, self.copies, self.buf = place, copies, buf
        self.base = copies.take(8)
        self.cut = buf.shape[2] // 2

    def slot(self, dz, other=0):
        c = self.p.c if other == 0 else 1 - self.p.c
        return ((self.p.z + dz + 4) % 4) * 2 + c

    def part(self, dz, half, other=0):
        s = self.slot(dz, other)
        if half is None:
            return self.buf.at[s]
        return self.buf.at[s, :, pl.ds(half * self.cut, self.cut)]

    EVENTS = ((0, None, 0), (0, None, 1), (0, None, -1), (-1, 0, 1), (-1, None, 0), (1, 1, -1), (1, None, 0), (2, None, 0))

    def start(self, *events):
        for ev in events:
            dz, half, way = self.EVENTS[ev]
            part = self.part(dz, half)
            dev = self.p.ring(way, self.p.c) if way else (self.p.tm, self.p.t + 1 - 2 * self.p.c)
            self.copies.start(part, part, self.base + ev, dev)

    def wait(self, *events):
        for ev in events:
            dz, half, way = self.EVENTS[ev]
            landed = self.part(dz - way, half) if way else self.part(dz, None, 1)
            dev = self.p.ring(way, self.p.c) if way else (self.p.tm, self.p.t + 1 - 2 * self.p.c)
            self.copies.arrived(landed, self.base + ev, dev)

    def first(self):
        self.start(0, 1, 2)

    def second(self):
        self.wait(1)
        self.start(3, 4)
        self.wait(2)
        self.start(5, 6)

    def third(self):
        self.wait(3, 5)
        self.start(7)


def dot(a, b):
    return jnp.dot(a, b, preferred_element_type=F32)


def nt_dot(a, b):
    return lax.dot_general(a, b, (((1,), (1,)), ((), ())), preferred_element_type=F32)


def iota(shape, dim):
    return lax.broadcasted_iota(jnp.int32, shape, dim)


def layer_kernel(
    frames, gain_attn, gain_mlp, bias, meta, w0, w1, w2, w3, w4, out,
    b0, b1, b2, b3, b4, spread, halo, wide, q_s, k_s, v_s, mix, mix_in, z_out, z_in, kept, stream,
    hid, pp, pp_in, ps, pr, own_sum, pall, outbox, meta_all,
    send_sems, recv_sems, local_sems, a2a_send, a2a_recv,
):
    p = Place()
    copies = Copies(send_sems, recv_sems)
    weights = RingGather(p, copies, (w0, w1, w2, w3, w4), (b0, b1, b2, b3, b4), local_sems)
    mate = (p.tm, p.t + 1 - 2 * p.c)

    def full(ref):
        return ref[...].reshape(DP, ref.shape[2])

    sem = pltpu.get_barrier_semaphore()
    cross = (1 - p.zl) * 2 + p.c

    @pl.loop(1, N_TM)
    def _(k):
        pl.semaphore_signal(sem, inc=1, device_id=((p.tm + k) % N_TM, p.t), device_id_type=MESH)

    for k in range(1, 4):
        for tm in (p.tm, p.partner):
            pl.semaphore_signal(sem, inc=1, device_id=(tm, (p.t + k) % 4), device_id_type=MESH)
    pl.semaphore_signal(
        sem, inc=1, device_id=((p.tm + 2 * p.zh - 1 + N_TM) % N_TM, cross), device_id_type=MESH
    )
    pl.semaphore_wait(sem, N_TM - 1 + 7)

    weights.tick(0)
    rows_c = pl.ds(pl.multiple_of(p.c * 128, 128), 128)
    rows_o = pl.ds(pl.multiple_of((1 - p.c) * 128, 128), 128)
    halo_sem = copies.take(4)
    below, above = ((p.tm + N_TM - 1) % N_TM, cross), ((p.tm + 1) % N_TM, cross)
    copies.start(frames.at[pl.ds(pl.multiple_of(p.c * 128, 128), 128)], halo.at[1, rows_c], halo_sem, below)
    copies.start(
        frames.at[pl.ds(pl.multiple_of(PATCHES + p.c * 128, 128), 128)], halo.at[0, rows_c], halo_sem + 1, above
    )
    meta_sem = copies.take()
    copies.start(meta, meta_all.at[p.zh], meta_sem, (p.partner, p.t))
    meta_all[p.zh] = meta[...]

    col = iota((1, DP), 1)
    target = jnp.where(col % PROWS < ROWS, col // PROWS * ROWS + col % PROWS, -1)

    @pl.loop(0, D // 128)
    def _(i):
        at = pl.ds(pl.multiple_of(i * 128, 128), 128)
        spread[at, :] = (iota((128, DP), 0) + i * 128 == target).astype(F32).astype(BF16)

    def norm_rows(values):
        values = values.astype(F32)
        centred = values - jnp.sum(values, axis=-1, keepdims=True) * (1.0 / D)
        var = jnp.sum(centred * centred, axis=-1, keepdims=True) * (1.0 / D)
        normed = (centred * lax.rsqrt(var + eps) * gain_attn[...]).astype(BF16)
        return dot(normed, spread[...]).astype(BF16)

    weights.tick(1)

    @pl.loop(0, 4)
    def _(i):
        at = pl.ds(pl.multiple_of(i * 128, 128), 128)
        wide[pl.ds(pl.multiple_of(PATCHES + i * 128, 128), 128), :] = norm_rows(frames[at, :])

    weights.tick(2)
    for i, dev in ((1, below), (0, above)):
        copies.arrived(halo.at[i, rows_c], halo_sem + 1 - i, dev)
        copies.start(halo.at[i, rows_c], halo.at[i, rows_c], halo_sem + 2 + i, mate)
    weights.tick(3)
    for i in range(2):
        copies.arrived(halo.at[i, rows_o], halo_sem + 2 + i, mate)

        @pl.loop(0, 2)
        def _(j, i=i):
            at = pl.ds(pl.multiple_of(j * 128, 128), 128)
            wide[pl.ds(pl.multiple_of(i * 3 * PATCHES + j * 128, 128), 128), :] = norm_rows(halo[i, at, :])

    for f in range(2):
        at = pl.ds(pl.multiple_of(f * PATCHES + p.t * BLK, BLK), BLK)
        stream[pl.ds(f * BLK, BLK), :] = dot(frames[at, :], spread[...])
    weights.tick(4)
    weights.tick(5)

    @pl.loop(0, 4)
    def _(i):
        at = pl.ds(pl.multiple_of(i * PATCHES, PATCHES), PATCHES)
        k_s[at, :] = dot(wide[at, :], b0[:, :, pl.ds(HW, HW)].reshape(DP, HW)).astype(BF16)
        v_s[at, :] = dot(wide[at, :], b0[:, :, pl.ds(2 * HW, HW)].reshape(DP, HW)).astype(BF16)

    @pl.loop(0, 2)
    def _(i):
        at = pl.ds(pl.multiple_of(i * PATCHES, PATCHES), PATCHES)
        src = pl.ds(pl.multiple_of((i + 1) * PATCHES, PATCHES), PATCHES)
        q_s[at, :] = dot(wide[src, :], b0[:, :, pl.ds(0, HW)].reshape(DP, HW)).astype(BF16)

    weights.tick(6)

    mix_sem = copies.take(6)
    scale = HEAD_DIM ** (-0.5)

    def attend(f):
        bias_rows = jnp.concatenate(
            [jnp.broadcast_to(bias[pl.ds(4 * f + b, 1), :], (BLK, 3 * PATCHES)) for b in range(4)], axis=0
        )
        keys = pl.ds(f * PATCHES, 3 * PATCHES)
        pieces = [jnp.zeros((PATCHES, 128), F32) for _ in range(3)]
        for h in range(HERE):
            lo, hi = h * HEAD_DIM, (h + 1) * HEAD_DIM
            first, last = lo // 128, (hi - 1) // 128
            n = (last - first + 1) * 128
            lanes = pl.ds(first * 128, n)
            lane = iota((PATCHES, n), 1) + first * 128
            mine = (lane >= lo) & (lane < hi)
            query = q_s[pl.ds(f * PATCHES, PATCHES), lanes].astype(F32)
            query = jnp.where(mine, query, 0.0).astype(BF16)
            scores = nt_dot(query, k_s[keys, lanes]) * scale + bias_rows
            expw = jnp.exp(scores - jnp.max(scores, axis=-1, keepdims=True))
            probs = (expw * (1.0 / jnp.sum(expw, axis=-1, keepdims=True))).astype(BF16)
            got = jnp.where(mine, dot(probs, v_s[keys, lanes]), 0.0)
            for j in range(first, last + 1):
                pieces[j] = pieces[j] + got[:, (j - first) * 128:(j - first + 1) * 128]
        attended = jnp.concatenate(pieces, axis=1).astype(BF16)
        return attended

    def mix_out(f, attended):
        for b in range(4):
            mix[f, b] = nt_dot(attended[b * BLK:(b + 1) * BLK], full(b1)).astype(BF16)
        for j in range(2):
            copies.start(mix.at[f, 2 * j + 1 - p.c], mix_in.at[f, j], mix_sem + 3 * f + j, mate)

    z_mate = (p.tm, (p.t + 2) % 4)

    def mix_sum(f):
        for j in range(2):
            copies.arrived(mix_in.at[f, j], mix_sem + 3 * f + j, mate)
        far = 1 - p.zl
        z_out[f] = (mix[f, 2 * far + p.c].astype(F32) + mix_in[f, far].astype(F32)).astype(BF16)
        copies.start(z_out.at[f], z_in.at[f], mix_sem + 3 * f + 2, z_mate)
        kept[f] = mix[f, 2 * p.zl + p.c].astype(F32) + mix_in[f, p.zl].astype(F32)

    attended = attend(0)
    weights.tick(7)
    mix_out(0, attended)
    attended = attend(1)
    mix_sum(0)
    weights.tick(8)
    mix_out(1, attended)
    weights.tick(9)
    mix_sum(1)

    hidden = ZRing(p, copies, hid)
    real = (col % PROWS < ROWS).astype(F32)
    for f in range(2):
        at = pl.ds(f * BLK, BLK)
        copies.arrived(z_in.at[f], mix_sem + 3 * f + 2, z_mate)
        rows = stream[at, :] + (kept[f] + z_in[f].astype(F32))
        stream[at, :] = rows
        centred = (rows - jnp.sum(rows, axis=-1, keepdims=True) * (1.0 / D)) * real
        var = jnp.sum(centred * centred, axis=-1, keepdims=True) * (1.0 / D)
        hid[hidden.slot(0), pl.ds(f * BLK, BLK), :] = (centred * lax.rsqrt(var + eps) * gain_mlp[...]).astype(BF16)
    hidden.first()
    copies.arrived(meta_all.at[1 - p.zh], meta_sem, (p.partner, p.t))
    weights.tick(10)
    weights.tick(11)

    part_sem = copies.take(4)
    ring_sem = copies.take(3)

    def chooser(zh, t):
        ids = meta_all[zh, pl.ds(t, 1), :]
        row, lane = iota((32, 128), 0), iota((32, 128), 1)
        return (jnp.broadcast_to(ids, (32, 128)) == row % 16) & (row // 16 == lane // BLK)

    def mlp(dz):
        z = (p.z + dz + 4) % 4
        rows = hid[pl.ds(z * 2, 2)].reshape(256, DP)
        up = dot(rows, full(b2))
        act = (0.5 * up * (1.0 + lax.erf(up * (0.5 ** 0.5)))).astype(BF16)
        down = nt_dot(act, full(b3)).astype(BF16)
        for c in range(2):
            choose = chooser(z // 2, (z % 2) * 2 + c).astype(F32).astype(BF16)
            pp[z, c] = dot(choose, down[c * 128:(c + 1) * 128]).astype(BF16)
        copies.start(pp.at[z, 1 - p.c], pp_in.at[z], part_sem + (dz + 1), mate)

    def pass_on(dz):
        z = (p.z + dz + 4) % 4
        copies.arrived(pp_in.at[z], part_sem + (dz + 1), mate)
        total = pp[z, p.c].astype(F32) + pp_in[z].astype(F32)
        if dz == 0:
            own_sum[...] = total
        else:
            k = {-1: 0, 1: 1, 2: 2}[dz]
            ps[k] = total.astype(BF16)
            copies.start(ps.at[k], pr.at[k], ring_sem + k, p.ring(dz, p.c))

    hidden.wait(0)
    mlp(0)
    hidden.second()
    weights.tick(12)
    pass_on(0)
    hidden.wait(4)
    mlp(-1)
    hidden.third()
    weights.tick(13)
    pass_on(-1)
    hidden.wait(6)
    mlp(1)
    pass_on(1)
    hidden.wait(7)
    mlp(2)
    pass_on(2)

    choose = chooser(p.zh, p.t).astype(F32)
    total = own_sum[...] + lax.dot_general(
        choose, stream[...], (((1,), (0,)), ((), ())), precision=lax.Precision.HIGHEST, preferred_element_type=F32
    )
    for k, dz in enumerate((-1, 1, 2)):
        copies.arrived(pr.at[k], ring_sem + k, p.ring(dz, p.c))
        total = total + pr[k].astype(F32)
    pooled = ZRing(p, copies, pall)
    pall[pooled.slot(0)] = (total * (1.0 / POOL)).astype(BF16)
    pooled.first()
    pooled.second()
    pooled.third()
    pooled.wait(0, 4, 6, 7)

    projected = dot(pall[...].reshape(256, DP), full(b4)).astype(BF16)
    for zh in range(2):
        dest = jnp.broadcast_to(meta_all[zh, pl.ds(4, 1), :], (256, 128))
        place = (iota((256, 128), 0) == dest).astype(F32).astype(BF16)
        slots = dot(place, projected[zh * 128:(zh + 1) * 128])
        outbox[:, zh] = slots.reshape(N_TM, 8, LM8).astype(BF16)

    def a2a(k, dst_tm, src_tm):
        cols = pl.ds(pl.multiple_of((src_tm % 2) * LM8, LM8), LM8)
        return pltpu.make_async_remote_copy(
            src_ref=outbox.at[dst_tm], dst_ref=out.at[src_tm // 2, :, :, cols],
            send_sem=a2a_send.at[k], recv_sem=a2a_recv.at[k],
            device_id=(dst_tm, p.t), device_id_type=MESH,
        )

    @pl.loop(1, N_TM)
    def _(k):
        a2a(k, (p.tm + k) % N_TM, p.tm).start()

    out[p.xy, :, :, pl.ds(pl.multiple_of(p.zh * LM8, LM8), LM8)] = outbox[p.tm]
    copies.drain()

    @pl.loop(1, N_TM)
    def _(k):
        a2a(k, (p.tm + k) % N_TM, (p.tm + N_TM - k) % N_TM).wait_recv()

    @pl.loop(1, N_TM)
    def _(k):
        a2a(k, (p.tm + k) % N_TM, p.tm).wait_send()


def layer(frames, gain_attn, gain_mlp, bias, meta, parts):
    vmem = pl.BlockSpec(memory_space=pltpu.VMEM)
    n_sems = 5 * (2 * N_EVENTS + 1) + 4 + 1 + 6 + 8 + 4 + 3 + 8
    V = pltpu.VMEM
    return pl.pallas_call(
        layer_kernel,
        out_shape=jax.ShapeDtypeStruct((N_TM // 2, 2, 8, 2 * LM8), BF16),
        in_specs=[vmem] * 10,
        out_specs=vmem,
        scratch_shapes=[V((N_TM, PROWS, n), BF16) for n in WIDTHS] + [
            V((D, DP), BF16),
            V((2, PATCHES, D), BF16),
            V((4 * PATCHES, DP), BF16),
            V((2 * PATCHES, HW), BF16),
            V((4 * PATCHES, HW), BF16),
            V((4 * PATCHES, HW), BF16),
            V((2, 4, BLK, DP), BF16),
            V((2, 2, BLK, DP), BF16),
            V((2, BLK, DP), BF16),
            V((2, BLK, DP), BF16),
            V((2, BLK, DP), F32),
            V((2 * BLK, DP), F32),
            V((8, 2 * BLK, DP), BF16),
            V((4, 2, 32, DP), BF16),
            V((4, 32, DP), BF16),
            V((3, 32, DP), BF16),
            V((3, 32, DP), BF16),
            V((32, DP), F32),
            V((8, 32, DP), BF16),
            V((N_TM, 2, 8, LM8), BF16),
            V((2, 8, 128), jnp.int32),
            pltpu.SemaphoreType.DMA((n_sems,)),
            pltpu.SemaphoreType.DMA((n_sems,)),
            pltpu.SemaphoreType.DMA((5,)),
            pltpu.SemaphoreType.DMA((N_TM,)),
            pltpu.SemaphoreType.DMA((N_TM,)),
        ],
        compiler_params=pltpu.CompilerParams(collective_id=0, has_side_effects=True, vmem_limit_bytes=60 << 20),
    )(frames, gain_attn, gain_mlp, bias, meta, *parts)


def body(
    frames, gain_attn, w_qkv, w_out, gain_mlp, w_up, w_down, w_proj, windows, pool_map, owners
):
    tm = lax.axis_index("tm")
    rows = ((0, PROWS - ROWS),)

    def halves(w):
        w = w.reshape(ROWS, 2, w.shape[1] // 2).transpose(1, 0, 2)
        return jnp.pad(w, ((0, 0),) + rows + ((0, 0),))

    parts = [
        jnp.pad(w_qkv, rows + ((0, 0), (0, HW - HERE * HEAD_DIM))).reshape(PROWS, 3 * HW),
        jnp.pad(w_out.T, rows + ((0, HW - HERE * HEAD_DIM),)),
        halves(w_up),
        halves(w_down.T),
        halves(w_proj),
    ]
    block = jnp.arange(8, dtype=jnp.int32)
    local = windows - tm * 8 + 4 - (block // 4 * 4)[:, None]
    key_block = jnp.arange(3 * PATCHES, dtype=jnp.int32) // BLK
    chosen = jnp.any(local[:, :, None] == key_block[None, None, :], axis=1)
    bias = jnp.where(chosen, 0.0, -1e30).astype(F32)
    ids = owners[:, 0]
    earlier = jnp.arange(128, dtype=jnp.int32)
    rank = jnp.sum(
        ((ids[:, None] == ids[None, :]) & (earlier[None, :] < earlier[:, None])).astype(jnp.int32), axis=1
    )
    dest = (ids * 8 + rank).reshape(2, 4, 16).transpose(1, 0, 2).reshape(1, 128)
    maps = pool_map.reshape(2, 4, BLK).transpose(1, 0, 2).reshape(4, 128)
    meta = jnp.concatenate([maps, dest, jnp.zeros((3, 128), jnp.int32)], axis=0)
    gain_wide = jnp.pad(gain_mlp.reshape(N_TM, ROWS), ((0, 0), (0, PROWS - ROWS))).reshape(1, DP)
    received = layer(frames, gain_attn.reshape(1, D), gain_wide, bias, meta, parts)
    return received.reshape(1, N_TM * 8, 2 * LM8)


def solution(mesh):
    placed = (
        P("tm", None),
        P(),
        P("tm", None, "tensor"),
        P("tensor", "tm"),
        P(),
        P("tm", "tensor"),
        P("tensor", "tm"),
        P("tm", "tensor"),
        P("tm", None),
        P("tm"),
        P("tm", None),
    )
    return jax.shard_map(
        body, mesh=mesh, in_specs=placed, out_specs=P("tm", None, "tensor"), check_vma=False
    )
```

```python
import functools

import jax
import jax.numpy as jnp
from jax import lax
from jax.experimental import pallas as pl
from jax.experimental.pallas import tpu as pltpu
from jax.sharding import PartitionSpec as P

D = 1408
HEADS = 16
PATCHES = 256
BLK = 64
WIN = 8
POOL = 4
N_TM = 32
HEAD_DIM = D // HEADS
HERE = 4
HW = 384
ROWS = D // N_TM
PROWS = 48
DP = N_TM * PROWS
FF8 = 768
LM8 = 512
WIDTHS = (3 * HW, HW, FF8, FF8, LM8)
QKV, OUT, UP, DOWN, PROJ = range(5)
START = (0, 2, 4, 6, 8)
BANDS = (0, 128, 384, 640, 896, 1024)

eps = 1e-06
MESH = pl.DeviceIdType.MESH
OFFSETS = (0, -1, 1, 2)
N_EVENTS = 20
F32 = jnp.float32
BF16 = jnp.bfloat16


class Place:
    def __init__(self):
        self.tm = lax.axis_index("tm")
        self.t = lax.axis_index("tensor")
        self.xy = self.tm // 2
        self.x = self.tm // 8
        self.y = self.xy % 4
        self.zh = self.tm % 2
        self.zl = self.t // 2
        self.c = self.t % 2
        self.z = self.zh * 2 + self.zl
        self.partner = self.tm + 1 - 2 * self.zh

    def ring(self, dz, c):
        z = (self.z + dz + 4) % 4
        return (self.xy * 2 + z // 2, (z % 2) * 2 + c)


class Copies:
    def __init__(self, send_sems, recv_sems):
        self.send_sems, self.recv_sems = send_sems, recv_sems
        self.used = 0
        self.sent = []

    def take(self, n=1):
        self.used += n
        return self.used - n

    def make(self, src, dst, sem, dev):
        return pltpu.make_async_remote_copy(
            src_ref=src, dst_ref=dst, send_sem=self.send_sems.at[sem], recv_sem=self.recv_sems.at[sem],
            device_id=dev, device_id_type=MESH,
        )

    def start(self, src, dst, sem, dev):
        copy = self.make(src, dst, sem, dev)
        copy.start()
        self.sent.append(copy)

    def arrived(self, landed, sem, dev):
        self.make(landed, landed, sem, dev).wait_recv()

    def drain(self):
        for copy in self.sent:
            copy.wait_send()
        self.sent = []


class RingGather:
    def __init__(self, place, copies, parts, bufs, local_sems):
        self.p, self.copies, self.parts, self.bufs, self.local_sems = place, copies, parts, bufs, local_sems
        self.base = [copies.take(2 * N_EVENTS + 1) for _ in parts]

    def own(self, c):
        return self.parts[c] if c < UP else self.parts[c].at[self.p.zh]

    def theirs(self, c):
        return self.parts[c] if c < UP else self.parts[c].at[1 - self.p.zh]

    def colour(self, fam):
        return self.p.zh if fam == 0 else 1 - self.p.zh

    def at(self, fam, a, b, z):
        k = self.colour(fam)
        dx = a * (1 - k) + b * k
        dy = a * k + b * (1 - k)
        return (((self.p.x + dx + 4) % 4) * 4 + (self.p.y + dy + 4) % 4) * 2 + z

    def part(self, c, fam, a, b, half):
        buf = self.bufs[c]
        slot = self.at(fam, a, b, self.colour(fam))
        if half is None:
            return buf.at[slot]
        n = buf.shape[2]
        cut = (n // 2 + 127) // 128 * 128
        return buf.at[slot, :, pl.ds(0, cut) if half == 0 else pl.ds(cut, n - cut)]

    def event(self, c, fam, ev):
        if ev < 4:
            a, b, half, da, db = ((0, 0, None, 1, 0), (0, 0, None, -1, 0), (-1, 0, 0, 1, 0), (1, 0, 1, -1, 0))[ev]
        else:
            off = OFFSETS[(ev - 4) // 4]
            a, b, half, da, db = (
                (off, 0, None, 0, 1), (off, 0, None, 0, -1), (off, -1, 0, 0, 1), (off, 1, 1, 0, -1)
            )[(ev - 4) % 4]
        dst = self.part(c, fam, a, b, half)
        src = self.own(c) if fam == 0 and a == 0 and b == 0 else dst
        landed = self.part(c, fam, a - da if a - da > -2 else 2, b - db if b - db > -2 else 2, half)
        sem = self.base[c] + fam * N_EVENTS + ev
        return src, dst, landed, sem, (self.at(fam, da, db, self.p.zh), self.p.t)

    def start(self, c, fam, *events):
        for ev in events:
            src, dst, _, sem, dev = self.event(c, fam, ev)
            self.copies.start(src, dst, sem, dev)

    def wait(self, c, fam, *events):
        for ev in events:
            _, _, landed, sem, dev = self.event(c, fam, ev)
            self.copies.arrived(landed, sem, dev)

    def stage(self, c, s):
        z_sem, z_dev = self.base[c] + 2 * N_EVENTS, (self.p.partner, self.p.t)
        if s < 2:
            local = pltpu.make_async_copy(self.own(c), self.bufs[c].at[self.p.tm], self.local_sems.at[c])
        if s == 0:
            self.copies.start(self.theirs(c), self.bufs[c].at[self.p.tm], z_sem, z_dev)
            self.start(c, 0, 0, 1, 4, 5)
            local.start()
        elif s == 1:
            self.copies.arrived(self.bufs[c].at[self.p.partner], z_sem, z_dev)
            self.start(c, 1, 0, 1, 4, 5)
            local.wait()
        else:
            for fam in range(2):
                if s == 2:
                    self.wait(c, fam, 0)
                    self.start(c, fam, 2, 8, 9)
                    self.wait(c, fam, 1)
                    self.start(c, fam, 3, 12, 13)
                    for ev in (4, 5):
                        self.wait(c, fam, ev)
                        self.start(c, fam, ev + 2)
                elif s == 3:
                    self.wait(c, fam, 2, 3)
                    self.start(c, fam, 16, 17)
                    for ev in (8, 9, 12, 13):
                        self.wait(c, fam, ev)
                        self.start(c, fam, ev + 2)
                elif s == 4:
                    for ev in (16, 17):
                        self.wait(c, fam, ev)
                        self.start(c, fam, ev + 2)
                else:
                    self.wait(c, fam, 6, 7, 10, 11, 14, 15, 18, 19)

    def tick(self, now):
        for c in range(5):
            if 0 <= now - START[c] < 6:
                self.stage(c, now - START[c])


class ZRing:
    def __init__(self, place, copies, buf, first, count):
        self.p, self.copies, self.buf = place, copies, buf
        self.rows = pl.ds(first, count)
        self.base = copies.take(8)
        self.cut = buf.shape[2] // 2

    def slot(self, dz, other=0):
        c = self.p.c if other == 0 else 1 - self.p.c
        return ((self.p.z + dz + 4) % 4) * 2 + c

    def part(self, dz, half, other=0):
        s = self.slot(dz, other)
        if half is None:
            return self.buf.at[s, self.rows]
        return self.buf.at[s, self.rows, pl.ds(half * self.cut, self.cut)]

    EVENTS = ((0, None, 0), (0, None, 1), (0, None, -1), (-1, 0, 1), (-1, None, 0), (1, 1, -1), (1, None, 0), (2, None, 0))

    def start(self, *events):
        for ev in events:
            dz, half, way = self.EVENTS[ev]
            part = self.part(dz, half)
            dev = self.p.ring(way, self.p.c) if way else (self.p.tm, self.p.t + 1 - 2 * self.p.c)
            self.copies.start(part, part, self.base + ev, dev)

    def wait(self, *events):
        for ev in events:
            dz, half, way = self.EVENTS[ev]
            landed = self.part(dz - way, half) if way else self.part(dz, None, 1)
            dev = self.p.ring(way, self.p.c) if way else (self.p.tm, self.p.t + 1 - 2 * self.p.c)
            self.copies.arrived(landed, self.base + ev, dev)

    def first(self):
        self.start(0, 1, 2)

    def second(self):
        self.wait(1)
        self.start(3, 4)
        self.wait(2)
        self.start(5, 6)

    def third(self):
        self.wait(3, 5)
        self.start(7)


def dot(a, b):
    return jnp.dot(a, b, preferred_element_type=F32)


def nt_dot(a, b):
    return lax.dot_general(a, b, (((1,), (1,)), ((), ())), preferred_element_type=F32)


def iota(shape, dim):
    return lax.broadcasted_iota(jnp.int32, shape, dim)


def layer_kernel(
    frames, gain_attn, gain_mlp, windows, pool_map, owners, w_qkv, w_out_t, w_up, w_down_t, w_proj, out,
    s0, s1, s2, s3, s4, b0, b1, b2, b3, b4, band, halo, wide, q_s, k_s, v_s, mix, mix_in, z_out, z_in, kept, stream,
    hid, pp, pp_in, ps, pr, own_sum, pall, outbox, meta, meta_all, bias, gain_row, gain_wide,
    send_sems, recv_sems, local_sems, a2a_send, a2a_recv,
):
    p = Place()
    copies = Copies(send_sems, recv_sems)
    weights = RingGather(p, copies, (s0, s1, s2, s3, s4), (b0, b1, b2, b3, b4), local_sems)
    mate = (p.tm, p.t + 1 - 2 * p.c)

    def full(ref):
        return ref[...].reshape(DP, ref.shape[2])

    sem = pltpu.get_barrier_semaphore()
    cross = (1 - p.zl) * 2 + p.c
    greeted = [(weights.at(0, a, b, p.zh), p.t) for a, b in ((1, 0), (-1, 0), (0, 1), (0, -1))]
    greeted += [(p.partner, p.t)]
    greeted += [(tm, (p.t + k) % 4) for k in range(1, 4) for tm in (p.tm, p.partner)]
    greeted += [((p.tm + 2 * p.zh - 1 + N_TM) % N_TM, cross)]
    for dev in greeted:
        pl.semaphore_signal(sem, inc=1, device_id=dev, device_id_type=MESH)

    wide_here = HERE * HEAD_DIM
    s0[...] = jnp.zeros((PROWS, 3 * HW), BF16)
    for j in range(3):
        s0[0:ROWS, j * HW:j * HW + wide_here] = w_qkv[j]
    pl.semaphore_wait(sem, len(greeted))
    weights.tick(0)
    s1[...] = jnp.zeros((PROWS, HW), BF16)
    s1[0:ROWS, 0:wide_here] = w_out_t[...]
    for st, w in ((s2, w_up), (s3, w_down_t), (s4, w_proj)):
        n = st.shape[2]
        for h in range(2):
            st[h] = jnp.zeros((PROWS, n), BF16)
            st[h, 0:ROWS, :] = w[:, h * n:(h + 1) * n]

    for j, first in enumerate(BANDS):
        col = iota((1, 256), 1) + j * 256
        target = jnp.where(col % PROWS < ROWS, col // PROWS * ROWS + col % PROWS, -1)
        band[j] = (iota((384, 256), 0) + first == target).astype(F32).astype(BF16)

    def spread(values):
        return jnp.concatenate(
            [dot(values[:, first:first + 384], band[j]) for j, first in enumerate(BANDS)], axis=1
        )

    gain_row[...] = jnp.concatenate([gain_attn[i:i + 1, :] for i in range(D // 128)], axis=1)

    def norm_rows(values):
        values = values.astype(F32)
        centred = values - jnp.sum(values, axis=-1, keepdims=True) * (1.0 / D)
        var = jnp.sum(centred * centred, axis=-1, keepdims=True) * (1.0 / D)
        normed = (centred * lax.rsqrt(var + eps) * gain_row[...]).astype(BF16)
        return spread(normed).astype(BF16)

    weights.tick(1)

    part = jnp.concatenate([gain_mlp[i:i + 1, :] for i in range(D // 128)], axis=1)
    gain = jnp.zeros((1, DP), F32)
    for _ in range(3):
        top = part.astype(BF16)
        gain = gain + spread(jnp.broadcast_to(top.astype(F32), (16, D)).astype(BF16))[0:1]
        part = part - top.astype(F32)
    gain_wide[...] = gain

    block = iota((8, 3 * PATCHES), 0)
    key_block = iota((8, 3 * PATCHES), 1) // BLK + p.tm * 8 - 4 + block // 4 * 4
    hits = jnp.zeros((8, 3 * PATCHES), jnp.int32)
    for j in range(WIN):
        hits = hits + (jnp.broadcast_to(windows[:, j:j + 1], (8, 3 * PATCHES)) == key_block).astype(jnp.int32)
    bias[...] = jnp.where(hits > 0, 0.0, -1e30).astype(F32)

    lane = iota((1, 128), 1)
    meta[...] = jnp.zeros((8, 128), jnp.int32)
    for t in range(4):
        f0, f1 = pool_map[t // 2:t // 2 + 1, :], pool_map[2 + t // 2:3 + t // 2, :]
        if t % 2 == 0:
            f1 = jnp.concatenate([f1[:, BLK:], f1[:, :BLK]], axis=1)
        else:
            f0 = jnp.concatenate([f0[:, BLK:], f0[:, :BLK]], axis=1)
        meta[t:t + 1, :] = jnp.where(lane < BLK, f0, f1)

    def natural(i):
        return (i // 16) % 2 * 64 + i // 32 * 16 + i % 16

    to, at_row = natural(iota((128, 128), 1)), iota((128, 128), 0)
    ids = jnp.broadcast_to(owners[...], (16, 128)).astype(F32).astype(BF16)
    ids = dot(ids, (at_row == to).astype(F32).astype(BF16))[0:1]
    wide_ids = jnp.broadcast_to(ids, (128, 128))
    before = (jnp.transpose(wide_ids) == wide_ids) & (natural(at_row) < to)
    rank = jnp.sum(before.astype(F32), axis=0, keepdims=True)
    meta[4:5, :] = (ids * 8.0 + rank).astype(jnp.int32)
    meta_sem = copies.take()
    meta_all[p.zh] = meta[...]

    rows_c = pl.ds(pl.multiple_of(p.c * 128, 128), 128)
    rows_o = pl.ds(pl.multiple_of((1 - p.c) * 128, 128), 128)
    halo_sem = copies.take(4)
    below, above = ((p.tm + N_TM - 1) % N_TM, cross), ((p.tm + 1) % N_TM, cross)
    weights.tick(2)
    copies.start(frames.at[pl.ds(pl.multiple_of(p.c * 128, 128), 128)], halo.at[1, rows_c], halo_sem, below)
    copies.start(
        frames.at[pl.ds(pl.multiple_of(PATCHES + p.c * 128, 128), 128)], halo.at[0, rows_c], halo_sem + 1, above
    )

    def norm_own(i):
        wide[pl.ds((i + 1) * PATCHES, PATCHES), :] = norm_rows(frames[pl.ds(i * PATCHES, PATCHES), :])

    norm_own(0)
    weights.tick(3)
    norm_own(1)
    copies.start(meta, meta_all.at[p.zh], meta_sem, (p.partner, p.t))
    weights.tick(4)

    for f in range(2):
        at = pl.ds(pl.multiple_of(f * PATCHES + p.t * BLK, BLK), BLK)
        stream[pl.ds(f * BLK, BLK), :] = spread(frames[at, :])
    weights.tick(5)

    own = dot(wide[pl.ds(PATCHES, 2 * PATCHES), :], full(b0)).astype(BF16)
    q_s[...] = own[:, :HW]
    k_s[pl.ds(PATCHES, 2 * PATCHES), :] = own[:, HW:2 * HW]
    v_s[pl.ds(PATCHES, 2 * PATCHES), :] = own[:, 2 * HW:]
    weights.tick(6)
    for i, dev in ((1, below), (0, above)):
        copies.arrived(halo.at[i, rows_c], halo_sem + 1 - i, dev)
        copies.start(halo.at[i, rows_c], halo.at[i, rows_c], halo_sem + 2 + i, mate)
    weights.tick(7)
    for i in range(2):
        copies.arrived(halo.at[i, rows_o], halo_sem + 2 + i, mate)

    @pl.loop(0, 2)
    def _(i):
        at = pl.ds(pl.multiple_of(i * 3 * PATCHES, PATCHES), PATCHES)
        normed = norm_rows(halo[i])
        got = dot(normed, b0[:, :, pl.ds(HW, 2 * HW)].reshape(DP, 2 * HW)).astype(BF16)
        k_s[at, :] = got[:, :HW]
        v_s[at, :] = got[:, HW:]

    weights.tick(8)

    mix_sem = copies.take(6)
    scale = HEAD_DIM ** (-0.5)

    def attend(f):
        bias_rows = jnp.concatenate(
            [jnp.broadcast_to(bias[pl.ds(4 * f + b, 1), :], (BLK, 3 * PATCHES)) for b in range(4)], axis=0
        )
        keys = pl.ds(f * PATCHES, 3 * PATCHES)
        pieces = [jnp.zeros((PATCHES, 128), F32) for _ in range(3)]
        for h in range(HERE):
            lo, hi = h * HEAD_DIM, (h + 1) * HEAD_DIM
            first, last = lo // 128, (hi - 1) // 128
            n = (last - first + 1) * 128
            lanes = pl.ds(first * 128, n)
            lane = iota((PATCHES, n), 1) + first * 128
            mine = (lane >= lo) & (lane < hi)
            query = q_s[pl.ds(f * PATCHES, PATCHES), lanes].astype(F32)
            query = jnp.where(mine, query, 0.0).astype(BF16)
            scores = nt_dot(query, k_s[keys, lanes]) * scale + bias_rows
            expw = jnp.exp(scores - jnp.max(scores, axis=-1, keepdims=True))
            probs = (expw * (1.0 / jnp.sum(expw, axis=-1, keepdims=True))).astype(BF16)
            got = jnp.where(mine, dot(probs, v_s[keys, lanes]), 0.0)
            for j in range(first, last + 1):
                pieces[j] = pieces[j] + got[:, (j - first) * 128:(j - first + 1) * 128]
        attended = jnp.concatenate(pieces, axis=1).astype(BF16)
        return attended

    def mix_out(f, attended):
        terms = nt_dot(attended, full(b1)).astype(BF16)
        for b in range(4):
            mix[f, b] = terms[b * BLK:(b + 1) * BLK]
        for j in range(2):
            copies.start(mix.at[f, 2 * j + 1 - p.c], mix_in.at[f, j], mix_sem + 3 * f + j, mate)

    z_mate = (p.tm, (p.t + 2) % 4)

    def mix_sum(f):
        for j in range(2):
            copies.arrived(mix_in.at[f, j], mix_sem + 3 * f + j, mate)
        far = 1 - p.zl
        z_out[f] = (mix[f, 2 * far + p.c].astype(F32) + mix_in[f, far].astype(F32)).astype(BF16)
        copies.start(z_out.at[f], z_in.at[f], mix_sem + 3 * f + 2, z_mate)
        kept[f] = mix[f, 2 * p.zl + p.c].astype(F32) + mix_in[f, p.zl].astype(F32)

    hidden = [ZRing(p, copies, hid, f * BLK, BLK) for f in range(2)]
    column = iota((1, DP), 1)
    real = (column % PROWS < ROWS).astype(F32)

    def second_norm(f):
        at = pl.ds(f * BLK, BLK)
        copies.arrived(z_in.at[f], mix_sem + 3 * f + 2, z_mate)
        rows = stream[at, :] + (kept[f] + z_in[f].astype(F32))
        stream[at, :] = rows
        centred = (rows - jnp.sum(rows, axis=-1, keepdims=True) * (1.0 / D)) * real
        var = jnp.sum(centred * centred, axis=-1, keepdims=True) * (1.0 / D)
        normed = (centred * lax.rsqrt(var + eps) * gain_wide[...]).astype(BF16)
        hid[hidden[f].slot(0), at, :] = normed
        hidden[f].first()

    mix_out(0, attend(0))
    weights.tick(9)
    mix_sum(0)
    attended = attend(1)
    weights.tick(10)
    mix_out(1, attended)
    second_norm(0)
    mix_sum(1)
    weights.tick(11)
    hidden[0].second()
    second_norm(1)
    copies.arrived(meta_all.at[1 - p.zh], meta_sem, (p.partner, p.t))
    weights.tick(12)
    hidden[0].third()

    part_sem = copies.take(4)
    ring_sem = copies.take(3)

    def chooser(zh, t):
        ids = meta_all[zh, pl.ds(t, 1), :]
        row, lane = iota((32, 128), 0), iota((32, 128), 1)
        return (jnp.broadcast_to(ids, (32, 128)) == row % 16) & (row // 16 == lane // BLK)

    def mlp(dz):
        z = (p.z + dz + 4) % 4
        rows = hid[pl.ds(z * 2, 2)].reshape(256, DP)
        up = dot(rows, full(b2))
        act = (0.5 * up * (1.0 + lax.erf(up * (0.5 ** 0.5)))).astype(BF16)
        down = nt_dot(act, full(b3)).astype(BF16)
        for c in range(2):
            choose = chooser(z // 2, (z % 2) * 2 + c).astype(F32).astype(BF16)
            pp[z, c] = dot(choose, down[c * 128:(c + 1) * 128]).astype(BF16)
        copies.start(pp.at[z, 1 - p.c], pp_in.at[z], part_sem + (dz + 1), mate)

    def pass_on(dz):
        z = (p.z + dz + 4) % 4
        copies.arrived(pp_in.at[z], part_sem + (dz + 1), mate)
        total = pp[z, p.c].astype(F32) + pp_in[z].astype(F32)
        if dz == 0:
            own_sum[...] = total
        else:
            k = {-1: 0, 1: 1, 2: 2}[dz]
            ps[k] = total.astype(BF16)
            copies.start(ps.at[k], pr.at[k], ring_sem + k, p.ring(dz, p.c))

    for f in range(2):
        hidden[f].wait(0)
    mlp(0)
    hidden[1].second()
    pass_on(0)
    for f in range(2):
        hidden[f].wait(4)
    mlp(-1)
    hidden[1].third()
    weights.tick(13)
    pass_on(-1)
    for f in range(2):
        hidden[f].wait(6)
    mlp(1)
    pass_on(1)
    for f in range(2):
        hidden[f].wait(7)
    mlp(2)
    pass_on(2)

    choose = chooser(p.zh, p.t).astype(F32)
    total = own_sum[...] + lax.dot_general(
        choose, stream[...], (((1,), (0,)), ((), ())), precision=lax.Precision.HIGHEST, preferred_element_type=F32
    )
    for k, dz in enumerate((-1, 1, 2)):
        copies.arrived(pr.at[k], ring_sem + k, p.ring(dz, p.c))
        total = total + pr[k].astype(F32)
    pooled = ZRing(p, copies, pall, 0, 32)
    pall[pooled.slot(0)] = (total * (1.0 / POOL)).astype(BF16)
    pooled.first()
    pooled.second()
    pooled.third()
    pooled.wait(0, 4, 6, 7)

    projected = dot(pall[...].reshape(256, DP), full(b4)).astype(BF16)
    for zh in range(2):
        dest = jnp.broadcast_to(meta_all[zh, pl.ds(4, 1), :], (256, 128))
        place = (iota((256, 128), 0) == dest).astype(F32).astype(BF16)
        slots = dot(place, projected[zh * 128:(zh + 1) * 128])
        outbox[:, zh] = slots.reshape(N_TM, 8, LM8).astype(BF16)

    def a2a(k, dst_tm, src_tm):
        cols = pl.ds(pl.multiple_of((src_tm % 2) * LM8, LM8), LM8)
        return pltpu.make_async_remote_copy(
            src_ref=outbox.at[dst_tm], dst_ref=out.at[src_tm // 2, :, :, cols],
            send_sem=a2a_send.at[k], recv_sem=a2a_recv.at[k],
            device_id=(dst_tm, p.t), device_id_type=MESH,
        )

    @pl.loop(1, N_TM)
    def _(k):
        a2a(k, (p.tm + k) % N_TM, p.tm).start()

    out[p.xy, :, :, pl.ds(pl.multiple_of(p.zh * LM8, LM8), LM8)] = outbox[p.tm]
    copies.drain()

    @pl.loop(1, N_TM)
    def _(k):
        a2a(k, (p.tm + k) % N_TM, (p.tm + N_TM - k) % N_TM).wait_recv()

    @pl.loop(1, N_TM)
    def _(k):
        a2a(k, (p.tm + k) % N_TM, p.tm).wait_send()


def layer(*args):
    vmem = pl.BlockSpec(memory_space=pltpu.VMEM)
    n_sems = 5 * (2 * N_EVENTS + 1) + 4 + 1 + 6 + 16 + 4 + 3 + 8
    V = pltpu.VMEM
    staged = [V((PROWS, n), BF16) if i < UP else V((2, PROWS, n), BF16) for i, n in enumerate(WIDTHS)]
    return pl.pallas_call(
        layer_kernel,
        out_shape=jax.ShapeDtypeStruct((N_TM // 2, 2, 8, 2 * LM8), BF16),
        in_specs=[vmem] * len(args),
        out_specs=vmem,
        scratch_shapes=staged + [V((N_TM, PROWS, n), BF16) for n in WIDTHS] + [
            V((6, 384, 256), BF16),
            V((2, PATCHES, D), BF16),
            V((3 * PATCHES, DP), BF16),
            V((2 * PATCHES, HW), BF16),
            V((4 * PATCHES, HW), BF16),
            V((4 * PATCHES, HW), BF16),
            V((2, 4, BLK, DP), BF16),
            V((2, 2, BLK, DP), BF16),
            V((2, BLK, DP), BF16),
            V((2, BLK, DP), BF16),
            V((2, BLK, DP), F32),
            V((2 * BLK, DP), F32),
            V((8, 2 * BLK, DP), BF16),
            V((4, 2, 32, DP), BF16),
            V((4, 32, DP), BF16),
            V((3, 32, DP), BF16),
            V((3, 32, DP), BF16),
            V((32, DP), F32),
            V((8, 32, DP), BF16),
            V((N_TM, 2, 8, LM8), BF16),
            V((8, 128), jnp.int32),
            V((2, 8, 128), jnp.int32),
            V((8, 3 * PATCHES), F32),
            V((1, D), F32),
            V((1, DP), F32),
            pltpu.SemaphoreType.DMA((n_sems,)),
            pltpu.SemaphoreType.DMA((n_sems,)),
            pltpu.SemaphoreType.DMA((5,)),
            pltpu.SemaphoreType.DMA((N_TM,)),
            pltpu.SemaphoreType.DMA((N_TM,)),
        ],
        compiler_params=pltpu.CompilerParams(collective_id=0, has_side_effects=True, vmem_limit_bytes=60 << 20),
    )(*args)


def body(
    frames, gain_attn, w_qkv, w_out, gain_mlp, w_up, w_down, w_proj, windows, pool_map, owners
):
    received = layer(
        frames, gain_attn.reshape(D // 128, 128), gain_mlp.reshape(D // 128, 128), windows,
        pool_map.reshape(4, 128), owners.reshape(1, 128),
        w_qkv.transpose(1, 0, 2), w_out.T, w_up, w_down.T, w_proj,
    )
    return received.reshape(1, N_TM * 8, 2 * LM8)


def solution(mesh):
    placed = (
        P("tm", None),
        P(),
        P("tm", None, "tensor"),
        P("tensor", "tm"),
        P(),
        P("tm", "tensor"),
        P("tensor", "tm"),
        P("tm", "tensor"),
        P("tm", None),
        P("tm"),
        P("tm", None),
    )
    return jax.shard_map(
        body, mesh=mesh, in_specs=placed, out_specs=P("tm", None, "tensor"), check_vma=False
    )
```
